512 devices in a mesh: segment: 2 (over core), dp: 64 (over y, z), rows: 4 (over x).
Axes of the slice: x: 4, y: 8, z: 8, core: 2. Of those that a mesh axis runs over, the one named last changes fastest.
Arguments:
- latent: bfloat16 [128, 16, 16, 320], P('dp', 'rows'), may hold values from -6 to 6
- hint: bfloat16 [128, 16, 16, 320], P('dp', 'rows'), may hold values from -6 to 6
- decoder_in: bfloat16 [128, 16, 16, 320], P('dp', 'rows'), may hold values from -6 to 6
- target: bfloat16 [128, 16, 16, 320], P('dp', 'rows'), may hold values from -6 to 6
- first_convs: bfloat16 [2, 2, 2880, 320], P('segment', None, 'dp'), may hold values from -0.109375 to 0.109375
- second_convs: bfloat16 [2, 2880, 320], P('segment', 'dp'), may hold values from -0.109375 to 0.109375
- pointwise_weights: bfloat16 [2, 2, 320, 320], P('segment', None, 'dp'), may hold values from -0.3125 to 0.3125
Outputs:
- grad_first: float32 [921600], P(('segment', 'dp', 'rows'))
- grad_zero: float32 [102400], P(('segment', 'dp', 'rows'))
The draws below stay inside these ranges and needn't reach their ends.
All inputs are finite; a program needn't handle non-finite values.
Results may differ from the reference program's by a relative error of at most 0.0095.
Values may be sent and summed in bfloat16 or wider, within the bound.
A program may use at most 64 MiB of HBM per device.

```python
import math
import jax
import jax.numpy as jnp
from jax import lax

C = 320
WC = 16
SAMPLES = 128
H = 16
N_SEGMENT = 2


def level_of(rng, extent, cuts, least, largest):
    gain, own = 1.0, jax.random.fold_in(rng, 6)
    for dim, blocks in cuts:
        heights = jnp.exp(jax.random.uniform(jax.random.fold_in(own, dim), (blocks,), jnp.float32, least / len(cuts), largest / len(cuts)))
        gain = gain * jnp.repeat(heights, extent[dim] // blocks).reshape([-1 if axis == dim else 1 for axis in range(len(extent))])
    return gain


def centred(own_key, dims, spread, most, cuts=(), dtype=jnp.bfloat16):
    loudness = level_of(own_key, dims, cuts, -0.22, 0.18) if cuts else 1.0
    values = jax.random.normal(own_key, dims, jnp.float32) * spread * loudness
    return jnp.minimum(jnp.maximum(values, -most), most).astype(dtype)


def setup_inputs(seed: int = 0) -> dict:
    streams_of = jax.random.split(jax.random.key(seed), 8)
    latent = centred(streams_of[0], (SAMPLES, H, WC, C), 1.0, 6.0, ((0, 64), (1, 4)))
    hint = centred(streams_of[1], (SAMPLES, H, WC, C), 1.0, 6.0, ((0, 64), (1, 4)))
    decoder_in = centred(streams_of[2], (SAMPLES, H, WC, C), 1.0, 6.0, ((0, 64), (1, 4)))
    target = centred(streams_of[3], (SAMPLES, H, WC, C), 1.0, 6.0, ((0, 64), (1, 4)))
    first_convs = centred(streams_of[4], (N_SEGMENT, 2, 9 * C, C), (9 * C) ** -0.5, 0.109375, ((0, 2), (2, 64)))
    second_convs = centred(streams_of[5], (N_SEGMENT, 9 * C, C), (9 * C) ** -0.5, 0.109375, ((0, 2), (1, 64)))
    pointwise_weights = centred(streams_of[6], (N_SEGMENT, 2, C, C), C ** -0.5, 0.3125, ((0, 2), (2, 64)))
    return {"latent": latent, "hint": hint, "decoder_in": decoder_in, "target": target, "first_convs": first_convs, "second_convs": second_convs, "pointwise_weights": pointwise_weights}


def conv_same(values, weight):
    kernel = weight.astype(jnp.float32).reshape(3, 3, weight.shape[0] // 9, weight.shape[1])
    return lax.conv_general_dilated(values.astype(jnp.float32), kernel, (1, 1), 'SAME', dimension_numbers=('NHWC', 'HWIO', 'NHWC'), precision=lax.Precision.HIGHEST)

def conv_back(values, weight):
    zeros = jnp.zeros(values.shape[:3] + (weight.shape[0] // 9,), jnp.float32)
    _, pullback = jax.vjp(lambda inner: conv_same(inner, weight), zeros)
    return pullback(values.astype(jnp.float32))[0]

def conv_weight_grad(inputs, cotangent, weight):
    _, pullback = jax.vjp(lambda kern: conv_same(inputs, kern), weight.astype(jnp.float32))
    return pullback(cotangent.astype(jnp.float32))[0]

def project(values, weight):
    flat = values.reshape(-1, values.shape[-1])
    return jnp.dot(flat, weight, preferred_element_type=jnp.float32).reshape(values.shape[:-1] + (weight.shape[1],))

def swish_slope(value):
    logistic = jax.nn.sigmoid(value)
    return logistic * (1.0 + value * (1.0 - logistic))

def reference(latent, hint, decoder_in, target, first_convs, second_convs, pointwise_weights):
    scale = 1.0 / math.sqrt(SAMPLES * H * WC)
    control_in = (latent.astype(jnp.float32) + project(hint, pointwise_weights[0, 0])).astype(jnp.bfloat16)
    enc_pre = conv_same(latent, first_convs[0, 0])
    enc_act = jax.nn.silu(enc_pre).astype(jnp.bfloat16)
    ctl_pre = conv_same(control_in, first_convs[0, 1])
    ctl_act = jax.nn.silu(ctl_pre).astype(jnp.bfloat16)
    control_out = (control_in.astype(jnp.float32) + conv_same(ctl_act, second_convs[0])).astype(jnp.bfloat16)
    control_proj = project(control_out, pointwise_weights[0, 1]).astype(jnp.bfloat16)
    skip = (latent.astype(jnp.float32) + conv_same(enc_act, first_convs[1, 0]) + control_proj.astype(jnp.float32)).astype(jnp.bfloat16)
    dec_pre = conv_same(decoder_in, first_convs[1, 1]) + conv_same(skip, second_convs[1])
    output = jax.nn.silu(dec_pre) + project(decoder_in, pointwise_weights[1, 0]) + project(skip, pointwise_weights[1, 1])
    error = (output - target.astype(jnp.float32)) * scale
    error_half = error.astype(jnp.bfloat16)
    dec_grad = (error * swish_slope(dec_pre)).astype(jnp.bfloat16)
    skip_grad = (conv_back(dec_grad, second_convs[1]) + project(error_half, pointwise_weights[1, 1].T)).astype(jnp.bfloat16)
    grad_zero = jnp.dot(control_out.reshape(-1, C).T, skip_grad.reshape(-1, C), preferred_element_type=jnp.float32)
    control_grad = project(skip_grad, pointwise_weights[0, 1].T).astype(jnp.bfloat16)
    first_grad = (conv_back(control_grad, second_convs[0]) * swish_slope(ctl_pre)).astype(jnp.bfloat16)
    grad_first = conv_weight_grad(control_in, first_grad, first_convs[0, 1])
    return (grad_first.reshape(-1), grad_zero.reshape(-1))
```

```python
import math

import jax
import jax.numpy as jnp
from jax import lax
from jax.experimental import pallas as pl
from jax.experimental.pallas import tpu as pltpu
from jax.sharding import PartitionSpec as P

F32 = jnp.float32
BF16 = jnp.bfloat16
C = 320
WC = 16
NX = 4
NR = 8
ROWS = 16
PAD = 3
FIRST_SLOTS = ((0, 14, 28, 42, 48), (0, 7, 21, 35, 48))
MESH = pl.DeviceIdType.MESH


def slope(value):
    logistic = 1.0 / (1.0 + jnp.exp(-value))
    return logistic * (1.0 + value * (1.0 - logistic))


def silu(value):
    return value / (1.0 + jnp.exp(-value))


def mm(left, right):
    return jnp.dot(left, right, preferred_element_type=F32)


def mm_t(left, right):
    return lax.dot_general(left, right, (((1,), (1,)), ((), ())), preferred_element_type=F32)


def flat(value):
    return value.reshape(-1, value.shape[-1])


def moved(value, by):
    count = value.shape[0]
    column = lax.broadcasted_iota(jnp.int32, value.shape, 0) & (WC - 1)
    rolled = pltpu.roll(value, by % count, 0)
    edge = 0 if by == 1 else WC - 1
    return jnp.where(column == edge, 0.0, rolled)


def conv(load, w_ref, chunk):
    parts = []
    for b in range(3):
        total = None
        for a in range(3):
            term = mm(load(a), w_ref[chunk, (3 * a + b) * C : (3 * a + b + 1) * C, :])
            total = term if total is None else total + term
        parts.append(total)
    return parts[1] + moved(parts[0], 1) + moved(parts[2], -1)


def conv_back(load, w_ref, chunk):
    parts = []
    for b in range(3):
        total = None
        for a in range(3):
            term = mm_t(load(a), w_ref[chunk, (3 * a + b) * C : (3 * a + b + 1) * C, :])
            total = term if total is None else total + term
        parts.append(total)
    return parts[1] + moved(parts[0], -1) + moved(parts[2], 1)


def inside(value, height, top):
    cell = lax.broadcasted_iota(jnp.int32, value.shape, 0)
    row = lax.rem(cell // WC, height) + top
    return jnp.where((row >= 0) & (row < ROWS), value, 0.0)


def kernel(
    lat_ref, hint_ref, dec_ref, tgt_ref, first_ref, second_ref, pwk_ref, out_ref,
    wbuf, pbuf, w_ref, pw_ref, tmp, tmp2, pwf,
    lat_all, in_all, cin_all, co_all, sg_all, fg_all,
    pre_own, act, eact, cow, cproj, skip_w, eh, dg, sgh, xsel, fgs, zs,
    slots, rsb, rsr, s2b, s2r,
    a_s, a_r, b_s, b_r, x_s, x_r, e_s, e_r, h_s, h_r, g_s, g_r,
    co_s, co_r, sg_s, sg_r, fg_s, fg_r, r1_s, r1_r, r2_s, r2_r,
):
    s = lax.axis_index("segment")
    d = lax.axis_index("dp")
    r = lax.axis_index("rows")
    zero = s == 0
    one = s == 1
    y = d // NR
    z = lax.rem(d, NR)
    pa = jnp.where(zero, z, y)
    pb = jnp.where(zero, y, z)
    own = 4 * r

    def dp_of(a, b):
        return jnp.where(zero, b * NR + a, a * NR + b)

    def ring(position, by):
        return lax.rem(position + by + NR, NR)

    def dev(a, b):
        return (s, dp_of(a, b), r)

    def row_of(k):
        return lax.rem(r + k, NX)

    def rcopy(src, dst, send, recv, device):
        return pltpu.make_async_remote_copy(
            src_ref=src, dst_ref=dst, send_sem=send, recv_sem=recv,
            device_id=device, device_id_type=MESH,
        )

    def arrived(dst, send, recv):
        rcopy(dst, dst, send, recv, (s, d, row_of(1))).wait_recv()

    for c, value in enumerate((first_ref[0, 1], first_ref[0, 0], second_ref[0])):
        wbuf[c, pb, pa, 0:45, :] = value
    pbuf[pb, pa] = pwk_ref[...]
    margin = jnp.zeros((2, PAD, WC, C), BF16)
    for ref in (lat_all, in_all, cin_all):
        ref[:, 0:PAD] = margin
        ref[:, ROWS + PAD : ROWS + 2 * PAD] = margin
    lat_all[:, pl.ds(own + PAD, 4)] = lat_ref[...]
    edge = jnp.zeros((2, 1, WC, C), BF16)
    for ref in (dg, sgh):
        ref[:, 0:1] = edge
        ref[:, 5:6] = edge

    @pl.when(zero)
    def _():
        in_all[:, pl.ds(own + PAD, 4)] = hint_ref[...]

    @pl.when(one)
    def _():
        in_all[:, pl.ds(own + PAD, 4)] = dec_ref[...]

    barrier = pltpu.get_barrier_semaphore()
    peers = [dev(ring(pa, k), pb) for k in range(1, NR)]
    peers += [dev(pa, ring(pb, k)) for k in range(1, NR)]
    for k in range(1, NX):
        peers += [(0, d, row_of(k)), (1, d, row_of(k))]
    peers += [(1 - s, d, r)]
    for peer in peers:
        pl.semaphore_signal(barrier, inc=1, device_id=peer, device_id_type=MESH)
    pl.semaphore_wait(barrier, len(peers))

    sends = []

    def stage_a(k):
        for way in range(2):
            if way and k > 3:
                continue
            sign = 1 if way == 0 else -1
            held = ring(pa, -sign * (k - 1))
            for i, (src, dst) in enumerate(
                ((pbuf.at[pb, held], pbuf.at[pb, held]), (wbuf.at[:, pb, held], wbuf.at[:, pb, held]))
            ):
                copy = rcopy(src, dst, a_s.at[i, way, k - 1], a_r.at[i, way, k - 1], dev(ring(pa, sign), pb))
                copy.start()
                sends.append(copy)

    def wait_a(k):
        for way in range(2):
            if way and k > 3:
                continue
            sign = 1 if way == 0 else -1
            got = ring(pa, -sign * k)
            arrived(pbuf.at[pb, got], a_s.at[0, way, k - 1], a_r.at[0, way, k - 1])
            arrived(wbuf.at[:, pb, got], a_s.at[1, way, k - 1], a_r.at[1, way, k - 1])

    def b_block(c, block, way, k):
        part = pl.ds(0, NR) if k < 4 else pl.ds(4 * way, 4)
        return pbuf.at[block, part] if c == 3 else wbuf.at[c, block, part]

    def stage_b(c, k):
        for way in range(2):
            sign = 1 if way == 0 else -1
            ref = b_block(c, ring(pb, -sign * (k - 1)), way, k)
            copy = rcopy(ref, ref, b_s.at[c, way, k - 1], b_r.at[c, way, k - 1], dev(pa, ring(pb, sign)))
            copy.start()
            sends.append(copy)

    def wait_b(c, k):
        for way in range(2):
            sign = 1 if way == 0 else -1
            ref = b_block(c, ring(pb, -sign * k), way, k)
            arrived(ref, b_s.at[c, way, k - 1], b_r.at[c, way, k - 1])

    stage_a(1)
    for i, ref in enumerate((lat_all, in_all)):
        for k in range(1, NX):
            mine = ref.at[:, pl.ds(own + PAD, 4)]
            copy = rcopy(mine, mine, x_s.at[i, k], x_r.at[i, k], (s, d, row_of(k)))
            copy.start()
            sends.append(copy)
    for k in range(2, 5):
        wait_a(k - 1)
        stage_a(k)
    wait_a(4)
    for c in (3, 0, 1):
        stage_b(c, 1)
    for c in (3, 0, 1):
        wait_b(c, 1)
        stage_b(c, 2)
    stage_b(2, 1)
    for c in (3, 0, 1):
        wait_b(c, 2)
        stage_b(c, 3)
    wait_b(2, 1)
    stage_b(2, 2)
    for c in (3, 0, 1):
        wait_b(c, 3)
        stage_b(c, 4)
    wait_b(2, 2)
    stage_b(2, 3)
    for i, ref in enumerate((lat_all, in_all)):
        for k in range(1, NX):
            theirs = ref.at[:, pl.ds(4 * row_of(NX - k) + PAD, 4)]
            arrived(theirs, x_s.at[i, k], x_r.at[i, k])

    def compact(c):
        @pl.loop(0, 4)
        def _(g):
            for j in range(16):
                index = g * 16 + j
                hi, lo = index // NR, lax.rem(index, NR)
                block = wbuf[c, jnp.where(zero, hi, lo), jnp.where(zero, lo, hi)]
                tmp[45 * j : 45 * j + 48, :] = block.astype(F32)
            w_ref[c, pl.ds(pl.multiple_of(g * 720, 16), 720), :] = tmp[0:720, :].astype(BF16)

    def compact_points():
        @pl.loop(0, NR)
        def _(g):
            for k in range(2):
                for j in range(NR):
                    block = pbuf[jnp.where(zero, g, j), jnp.where(zero, j, g)]
                    tmp2[k, 5 * j : 5 * j + 8, :] = block.astype(F32)[8 * k : 8 * k + 8]
                pwf[k, pl.ds(pl.multiple_of(g * 40, 8), 40), :] = tmp2[k, 0:40, :]
        pw_ref[...] = pwf[...].astype(BF16)

    other = (1 - s, d, r)

    wait_b(3, 4)
    compact_points()

    @pl.when(zero)
    def _():
        mixed = mm(flat(in_all[:, PAD : ROWS + PAD]), pw_ref[0])
        mixed = mixed + flat(lat_all[:, PAD : ROWS + PAD]).astype(F32)
        cin_all[:, PAD : ROWS + PAD] = mixed.astype(BF16).reshape(2, ROWS, WC, C)
        body = cin_all.at[:, PAD : ROWS + PAD]
        rcopy(body, body, e_s.at[0], e_r.at[0], other).start()

    wait_b(0, 4)
    compact(0)

    @pl.when(zero)
    def _():
        pre = conv(lambda a: flat(cin_all[:, pl.ds(own + a, 8)]), w_ref, 0)
        kept = pre.reshape(2, 8, WC, C)
        pre_own[...] = kept[:, 2:6]
        act[...] = inside(silu(pre), 8, own - 2).astype(BF16).reshape(2, 8, WC, C)

    @pl.when(one)
    def _():
        pre = conv(lambda a: flat(in_all[:, pl.ds(own + PAD - 1 + a, 4)]), w_ref, 0)
        pre_own[...] = pre.reshape(2, 4, WC, C)

    wait_b(2, 3)
    stage_b(2, 4)
    wait_b(1, 4)
    compact(1)

    @pl.when(zero)
    def _():
        pre = conv(lambda a: flat(lat_all[:, pl.ds(own + a, 8)]), w_ref, 1)
        eact[...] = inside(silu(pre), 8, own - 2).astype(BF16).reshape(2, 8, WC, C)
        rcopy(eact, eact, e_s.at[1], e_r.at[1], other).start()

    wait_b(2, 4)
    compact(2)

    def select_first():
        for tap in range(5):
            line = jnp.where(zero, tap // 3, (4 + tap) // 3)
            start = jnp.where(zero, FIRST_SLOTS[0][tap], FIRST_SLOTS[1][tap])
            m = lax.broadcasted_iota(jnp.int32, (128, C), 0)
            c = lax.broadcasted_iota(jnp.int32, (128, C), 1)
            row = ((180 * (start + (m >> 3)) + 45 * r) >> 3) + (m & 7) - (C * tap - 160 * s)
            pick = jnp.where((c == row) & ((m & 7) < 7), 1.0, 0.0).astype(BF16)
            held = flat(cin_all[:, pl.ds(line + PAD - 1, ROWS)])
            xsel[tap] = mm_t(pick, held).astype(BF16)

    def spread(ref, send, recv):
        copies = []
        mine = ref.at[:, pl.ds(own, 4)]
        for k in range(1, NX):
            for core in range(2):
                copies.append(rcopy(mine, mine, send.at[k, core], recv.at[k], (core, d, row_of(k))))
        copies.append(rcopy(mine, mine, send.at[0, 0], recv.at[0], other))
        return copies

    def gathered(ref, send, recv, source):
        for k in range(1, NX):
            arrived(ref.at[:, pl.ds(4 * row_of(NX - k), 4)], send.at[k, 0], recv.at[k])

        @pl.when(s != source)
        def _():
            arrived(ref.at[:, pl.ds(own, 4)], send.at[0, 0], recv.at[0])

    @pl.when(zero)
    def _():
        total = conv(lambda a: flat(act[:, a : a + 6]), w_ref, 2)
        total = total + flat(cin_all[:, pl.ds(own + PAD - 1, 6)]).astype(F32)
        out = total.astype(BF16)
        cow[...] = out.reshape(2, 6, WC, C)
        cproj[...] = mm(out, pw_ref[1]).astype(BF16).reshape(2, 6, WC, C)
        rcopy(cproj, cproj, e_s.at[2], e_r.at[2], other).start()
        co_all[:, pl.ds(own, 4)] = cow[:, 1:5]
        for copy in spread(co_all, co_s, co_r):
            copy.start()
        select_first()

    def to_halo(k):
        src = dg.at[:, 1:2] if k < 0 else dg.at[:, 4:5]
        dst = dg.at[:, 5:6] if k < 0 else dg.at[:, 0:1]
        i = 0 if k < 0 else 1
        return rcopy(src, dst, h_s.at[i], h_r.at[i], (s, d, r + k))

    def to_control(k):
        mine = pl.ds(own, 4) if k == 0 else pl.ds(own, 1) if k < 0 else pl.ds(own + 3, 1)
        dst = sgh.at[:, 1:5] if k == 0 else sgh.at[:, 5:6] if k < 0 else sgh.at[:, 0:1]
        return rcopy(sg_all.at[:, mine], dst, g_s.at[k + 1], g_r.at[k + 1], (0, d, r + k))

    @pl.when(one)
    def _():
        arrived(eact, e_s.at[1], e_r.at[1])
        total = conv(lambda a: flat(eact[:, a : a + 6]), w_ref, 1)
        total = total + flat(lat_all[:, pl.ds(own + PAD - 1, 6)]).astype(F32)
        arrived(cproj, e_s.at[2], e_r.at[2])
        total = total + flat(cproj[...]).astype(F32)
        skip = inside(total, 6, own - 1).astype(BF16)
        skip_w[...] = skip.reshape(2, 6, WC, C)
        pre = flat(pre_own[...]) + conv(lambda a: flat(skip_w[:, a : a + 4]), w_ref, 2)
        output = silu(pre) + mm(flat(in_all[:, pl.ds(own + PAD, 4)]), pw_ref[0])
        output = output + mm(flat(skip_w[:, 1:5]), pw_ref[1])
        error = (output - flat(tgt_ref[...]).astype(F32)) * (1.0 / math.sqrt(128 * ROWS * WC))
        eh[...] = error.astype(BF16)
        dg[:, 1:5] = (error * slope(pre)).astype(BF16).reshape(2, 4, WC, C)
        for k in (-1, 1):
            @pl.when((r + k >= 0) & (r + k < NX))
            def _():
                to_halo(k).start()

        @pl.when(r < NX - 1)
        def _():
            arrived(dg.at[:, 5:6], h_s.at[0], h_r.at[0])

        @pl.when(r > 0)
        def _():
            arrived(dg.at[:, 0:1], h_s.at[1], h_r.at[1])

        back = conv_back(lambda a: flat(dg[:, 2 - a : 6 - a]), w_ref, 2)
        back = back + mm_t(eh[...], pw_ref[1])
        sg_all[:, pl.ds(own, 4)] = back.astype(BF16).reshape(2, 4, WC, C)
        to_control(0).start()
        for k in (-1, 1):
            @pl.when((r + k >= 0) & (r + k < NX))
            def _():
                to_control(k).start()
        for copy in spread(sg_all, sg_s, sg_r):
            copy.start()
        arrived(cin_all.at[:, PAD : ROWS + PAD], e_s.at[0], e_r.at[0])
        select_first()

    @pl.when(zero)
    def _():
        arrived(sgh.at[:, 1:5], g_s.at[1], g_r.at[1])

        @pl.when(r < NX - 1)
        def _():
            arrived(sgh.at[:, 5:6], g_s.at[0], g_r.at[0])

        @pl.when(r > 0)
        def _():
            arrived(sgh.at[:, 0:1], g_s.at[2], g_r.at[2])

        act[:, 0:6] = mm_t(flat(sgh[...]), pw_ref[1]).astype(BF16).reshape(2, 6, WC, C)
        back = conv_back(lambda a: flat(act[:, 2 - a : 6 - a]), w_ref, 2)
        grad = back * slope(flat(pre_own[...]))
        fg_all[:, pl.ds(own, 4)] = grad.astype(BF16).reshape(2, 4, WC, C)
        for copy in spread(fg_all, fg_s, fg_r):
            copy.start()

    gathered(co_all, co_s, co_r, 0)
    gathered(sg_all, sg_s, sg_r, 1)
    m = lax.broadcasted_iota(jnp.int32, (128, C), 0)
    c = lax.broadcasted_iota(jnp.int32, (128, C), 1)
    row = 160 * s + ((20 * (m & 63) + 5 * r) >> 3) + (m >> 6)
    pick = jnp.where(c == row, 1.0, 0.0).astype(BF16)
    picked = mm_t(pick, flat(co_all[...])).astype(BF16)
    both = mm(picked, flat(sg_all[...]))
    m = lax.broadcasted_iota(jnp.int32, (64, C), 0)
    lane = lax.broadcasted_iota(jnp.int32, (64, C), 1)
    zs[...] = jnp.where(lane >= 40 * ((4 * m + 5 * r) & 7), both[0:64], both[64:128])
    slots[...] = jnp.zeros(slots.shape, F32)
    for i in range(64):
        slots[i, 7:8, :] = zs[i : i + 1, :]

    gathered(fg_all, fg_s, fg_r, 0)
    whole = flat(fg_all[...])
    wide = whole.astype(F32)
    fgs[1] = whole
    fgs[0] = moved(wide, -1).astype(BF16)
    fgs[2] = moved(wide, 1).astype(BF16)
    for tap in range(5):
        column = jnp.where(zero, tap % 3, (4 + tap) % 3)
        start = jnp.where(zero, FIRST_SLOTS[0][tap], FIRST_SLOTS[1][tap])
        block = mm(xsel[tap], fgs[column])
        slots[pl.ds(start, 16)] += block.reshape(16, NR, C)

    @pl.when(zero)
    def _():
        for a in range(NR):
            part = jnp.concatenate([slots[NR * b + a] for b in range(NR)], axis=0)
            rsb[a] = part.astype(BF16)

    @pl.when(one)
    def _():
        for a in range(NR):
            part = jnp.concatenate([slots[NR * a + b] for b in range(NR)], axis=0)
            rsb[a] = part.astype(BF16)

    for k in range(1, NR):
        to = ring(pa, k)
        copy = rcopy(rsb.at[to], rsr.at[k], r1_s.at[k], r1_r.at[k], dev(to, pb))
        copy.start()
        sends.append(copy)
    total = rsb[pa].astype(F32)
    for k in range(1, NR):
        arrived(rsr.at[k], r1_s.at[k], r1_r.at[k])
        total = total + rsr[k].astype(F32)
    s2b[...] = total.reshape(NR, NR, C)
    for k in range(1, NR):
        to = ring(pb, k)
        copy = rcopy(s2b.at[to], s2r.at[k], r2_s.at[k], r2_r.at[k], dev(pa, to))
        copy.start()
        sends.append(copy)
    total = s2b[pb]
    for k in range(1, NR):
        arrived(s2r.at[k], r2_s.at[k], r2_r.at[k])
        total = total + s2r[k]
    out_ref[...] = total

    for copy in sends:
        copy.wait_send()

    @pl.when(zero)
    def _():
        body = cin_all.at[:, PAD : ROWS + PAD]
        for i, ref in enumerate((body, eact, cproj)):
            rcopy(ref, ref, e_s.at[i], e_r.at[i], other).wait_send()
        for copy in spread(co_all, co_s, co_r) + spread(fg_all, fg_s, fg_r):
            copy.wait_send()

    @pl.when(one)
    def _():
        to_control(0).wait_send()
        for k in (-1, 1):
            @pl.when((r + k >= 0) & (r + k < NX))
            def _():
                to_halo(k).wait_send()
                to_control(k).wait_send()
        for copy in spread(sg_all, sg_s, sg_r):
            copy.wait_send()


def per_device(latent, hint, decoder_in, target, first_convs, second_convs, pointwise):
    pwk = jnp.pad(pointwise[0], ((0, 0), (0, 3), (0, 0))).reshape(16, C)
    full = (2, ROWS, WC, C)
    padded = (2, ROWS + 2 * PAD, WC, C)
    vm = pltpu.VMEM
    dma = pltpu.SemaphoreType.DMA
    scratch = [
        vm((3, NR, NR, 48, C), BF16), vm((NR, NR, 16, C), BF16), vm((3, 9 * C, C), BF16),
        vm((2, C, C), BF16), vm((728, C), F32), vm((2, 48, C), F32), vm((2, C, C), F32),
        vm(padded, BF16), vm(padded, BF16), vm(padded, BF16), vm(full, BF16), vm(full, BF16), vm(full, BF16),
        vm((2, 4, WC, C), F32), vm((2, 8, WC, C), BF16), vm((2, 8, WC, C), BF16), vm((2, 6, WC, C), BF16),
        vm((2, 6, WC, C), BF16), vm((2, 6, WC, C), BF16), vm((128, C), BF16), vm((2, 6, WC, C), BF16),
        vm((2, 6, WC, C), BF16), vm((5, 128, 512), BF16), vm((3, 512, C), BF16), vm((64, C), F32),
        vm((64, NR, C), F32), vm((NR, 64, C), BF16), vm((NR, 64, C), BF16), vm((NR, NR, C), F32), vm((NR, NR, C), F32),
        dma((2, 2, 4)), dma((2, 2, 4)), dma((4, 2, 4)), dma((4, 2, 4)), dma((2, 4)), dma((2, 4)),
        dma((3,)), dma((3,)), dma((2,)), dma((2,)), dma((3,)), dma((3,)),
        dma((4, 2)), dma((4,)), dma((4, 2)), dma((4,)), dma((4, 2)), dma((4,)),
        dma((NR,)), dma((NR,)), dma((NR,)), dma((NR,)),
    ]
    got = pl.pallas_call(
        kernel,
        out_shape=jax.ShapeDtypeStruct((8, C), F32),
        in_specs=[pl.BlockSpec(memory_space=pltpu.VMEM)] * 7,
        out_specs=pl.BlockSpec(memory_space=pltpu.VMEM),
        scratch_shapes=scratch,
        compiler_params=pltpu.CompilerParams(
            collective_id=0, has_side_effects=True, vmem_limit_bytes=56 * 1024 * 1024
        ),
        name="step",
    )(latent, hint, decoder_in, target, first_convs, second_convs, pwk)
    d = lax.axis_index("dp")
    r = lax.axis_index("rows")
    offset = 40 * ((4 * d + 5 * r) & 7)
    first = lax.dynamic_slice(got[:7].reshape(-1), (offset,), (1800,))
    last = got[7]
    second = lax.dynamic_slice(jnp.concatenate([last, last]), (offset,), (200,))
    return first, second


def solution(mesh):
    placed = (
        P("dp", "rows", None, None),
        P("dp", "rows", None, None),
        P("dp", "rows", None, None),
        P("dp", "rows", None, None),
        P("segment", None, "dp", None),
        P("segment", "dp", None),
        P("segment", None, "dp", None),
    )
    return jax.shard_map(
        per_device,
        mesh=mesh,
        in_specs=placed,
        out_specs=(P(("segment", "dp", "rows")), P(("segment", "dp", "rows"))),
        check_vma=False,
    )
```

```python
import math

import jax
import jax.numpy as jnp
from jax import lax
from jax.experimental import pallas as pl
from jax.experimental.pallas import tpu as pltpu
from jax.sharding import PartitionSpec as P

F32 = jnp.float32
BF16 = jnp.bfloat16
C = 320
WC = 16
NX = 4
NR = 8
ROWS = 16
CELLS = ROWS * WC
HEIGHTS = (64, 48, 48)
ALONE = (2, 2, 2)
FIRST_SLOTS = ((0, 14, 28, 42, 48), (0, 7, 21, 35, 48))
MESH = pl.DeviceIdType.MESH


def slope(value):
    logistic = 1.0 / (1.0 + jnp.exp(-value))
    return logistic * (1.0 + value * (1.0 - logistic))


def silu(value):
    return value / (1.0 + jnp.exp(-value))


def mm(left, right):
    return jnp.dot(left, right, preferred_element_type=F32)


def mm_t(left, right):
    return lax.dot_general(left, right, (((1,), (1,)), ((), ())), preferred_element_type=F32)


def flat(value):
    return value.reshape(-1, value.shape[-1])


def moved(value, by):
    count = value.shape[0]
    column = lax.broadcasted_iota(jnp.int32, value.shape, 0) & (WC - 1)
    rolled = pltpu.roll(value, by % count, 0)
    edge = 0 if by == 1 else WC - 1
    return jnp.where(column == edge, 0.0, rolled)


def taps(load, w_ref, segment, chunk, product):
    parts = []
    for b in range(3):
        total = None
        for a in range(3):
            term = product(load(a), w_ref[segment, chunk, (3 * a + b) * C : (3 * a + b + 1) * C, :])
            total = term if total is None else total + term
        parts.append(total)
    return parts


def conv(ref, w_ref, segment, chunk):
    parts = taps(lambda a: flat(ref[a : a + ROWS]), w_ref, segment, chunk, mm)
    return parts[1] + moved(parts[0], 1) + moved(parts[2], -1)


def conv_back(ref, w_ref, segment, chunk):
    parts = taps(lambda a: flat(ref[2 - a : 2 - a + ROWS]), w_ref, segment, chunk, mm_t)
    return parts[1] + moved(parts[0], -1) + moved(parts[2], 1)


def place(by):
    if by == 0:
        return 0
    return 7 if abs(by) == 4 else 2 * by if by > 0 else -2 * by - 1


def kernel(
    lat_ref, hint_ref, dec_ref, tgt_ref, first_ref, second_ref, pwk_ref, out_ref,
    buf0, buf1, buf2, w_ref, pw_ref, tmp, tmp2, pwf,
    xin, cin2, co2, sg2, fg2, pre_c, pre_d, base, act, eact, skip_p, dg, xsel, fgs, zs,
    slots, rsb, rsr, s2b, s2r,
    a_s, a_r, b_s, b_r, x_s, x_r, d_s, d_r, i_s, i_r, e_s, e_r, r1_s, r1_r, r2_s, r2_r,
):
    s = lax.axis_index("segment")
    d = lax.axis_index("dp")
    r = lax.axis_index("rows")
    zero = s == 0
    y = d // NR
    z = lax.rem(d, NR)
    pa = jnp.where(zero, z, y)
    pb = jnp.where(zero, y, z)
    odd = lax.rem(r, 2)
    own = 4 * r
    bufs = (buf0, buf1, buf2)

    def ring(position, by):
        return lax.rem(position + by + NR, NR)

    def dev(by_a, by_b):
        a, b = ring(pa, by_a), ring(pb, by_b)
        return (s, jnp.where(zero, b * NR + a, a * NR + b), r)

    def row_of(k):
        return lax.rem(r + k + NX, NX)

    other = (1 - s, d, r)
    sends = []

    def rcopy(src, dst, send, recv, device):
        return pltpu.make_async_remote_copy(
            src_ref=src, dst_ref=dst, send_sem=send, recv_sem=recv,
            device_id=device, device_id_type=MESH,
        )

    def push(src, dst, send, recv, device):
        copy = rcopy(src, dst, send, recv, device)
        copy.start()
        sends.append(copy)

    def arrived(dst, send, recv):
        rcopy(dst, dst, send, recv, other).wait_recv()

    buf0[0, 0, 0, 0:45, :] = first_ref[0, 1]
    buf0[0, 0, 0, 48:64, :] = pwk_ref[...]
    buf1[0, 0, 0, 0:45, :] = first_ref[0, 0]
    buf2[0, 0, 0, 0:45, :] = second_ref[0]
    edge = jnp.zeros((1, WC, C), BF16)
    for ref in [xin.at[0], xin.at[2], cin2.at[0], cin2.at[1], act, eact, skip_p, dg]:
        ref[0:1] = edge
        ref[ROWS + 1 : ROWS + 2] = edge
    for i, ref in enumerate((lat_ref, hint_ref, dec_ref, tgt_ref)):
        xin[i, pl.ds(own + 1, 4)] = ref[s]

    barrier = pltpu.get_barrier_semaphore()
    peers = [dev(k, 0) for k in range(1, NR)] + [dev(0, k) for k in range(1, NR)]
    peers += [(s, d, row_of(k)) for k in range(1, NX)] + [other]
    for peer in peers:
        pl.semaphore_signal(barrier, inc=1, device_id=peer, device_id_type=MESH)
    pl.semaphore_wait(barrier, len(peers))

    def a_part(c, k, way):
        return bufs[c].at[0, 0, place(k if way else -k)]

    def send_a(c, k):
        for way in range(2 if k < 4 else 1):
            push(a_part(c, k - 1, way), a_part(c, k, way), a_s.at[c, way, k - 1], a_r.at[c, way, k - 1], dev(-1 if way else 1, 0))

    def wait_a(c, k):
        for way in range(2 if k < 4 else 1):
            arrived(a_part(c, k, way), a_s.at[c, way, k - 1], a_r.at[c, way, k - 1])

    def mine(c):
        return pl.ds(ALONE[c] * odd, ALONE[c])

    def theirs(c):
        return pl.ds(ALONE[c] * (1 - odd), ALONE[c])

    def both(c):
        return pl.ds(2 * ALONE[c], NR - 2 * ALONE[c])

    def ways(part, k):
        return (0, 1) if k < 4 else (part,)

    def b_part(c, part, k, way):
        which = mine(c) if part else both(c)
        return bufs[c].at[0, place(k if way else -k), which]

    def send_b(c, part, k):
        for way in ways(part, k):
            push(
                b_part(c, part, k - 1, way), b_part(c, part, k, way),
                b_s.at[c, part, way, k - 1], b_r.at[c, part, way, k - 1], dev(0, -1 if way else 1),
            )

    def wait_b(c, part, k):
        for way in ways(part, k):
            arrived(b_part(c, part, k, way), b_s.at[c, part, way, k - 1], b_r.at[c, part, way, k - 1])

    def send_x(c, k):
        for way in ways(1, k):
            ref = b_part(c, 1, k, way)
            push(ref, ref, x_s.at[c, way, k - 1], x_r.at[c, way, k - 1], (s, d, row_of(-1 if way else 1)))

    def wait_x(c, k):
        for way in ways(1, k):
            ref = bufs[c].at[0, place(k if way else -k), theirs(c)]
            arrived(ref, x_s.at[c, way, k - 1], x_r.at[c, way, k - 1])

    def span(k):
        return pl.ds(0, 1) if k == 0 else pl.ds(7, 1) if k == 4 else pl.ds(2 * k - 1, 2)

    def send_d(c, k):
        push(bufs[c].at[0, span(k)], bufs[c].at[1, span(k)], d_s.at[c, k], d_r.at[c, k], other)

    def wait_d(c):
        for k in range(5):
            arrived(bufs[c].at[1, span(k)], d_s.at[c, k], d_r.at[c, k])

    def turn(i, c):
        if i == 0:
            send_a(c, 1)
        elif i == 1:
            wait_a(c, 1)
            send_a(c, 2)
        elif i == 2:
            wait_a(c, 2)
            send_a(c, 3)
            send_b(c, 1, 1)
        elif i == 3:
            wait_a(c, 3)
            send_a(c, 4)
            wait_b(c, 1, 1)
            send_b(c, 1, 2)
            send_x(c, 1)
        elif i == 4:
            wait_a(c, 4)
            send_b(c, 0, 1)
            send_d(c, 0)
        elif i in (5, 7, 9):
            k = (i - 1) // 2
            wait_b(c, 1, k)
            if k < 4:
                send_b(c, 1, k + 1)
            send_x(c, k)
        elif i in (6, 8, 10):
            k = (i - 4) // 2
            wait_b(c, 0, k)
            send_b(c, 0, k + 1)
            wait_x(c, k)
            send_d(c, k)
        elif i == 11:
            wait_b(c, 0, 4)
            wait_x(c, 4)
            send_d(c, 4)

    for c in range(3):
        turn(0, c)
    part = xin.at[:, pl.ds(own + 1, 4)]
    for k in range(1, NX):
        push(part, part, i_s.at[k], i_r.at[k], (s, d, row_of(k)))
    lag = 3
    for i in range(1, 12):
        if i == 4:
            pass
        if i == 8:
            pass
        for c in (0, 1):
            turn(i, c)
        if 0 < i - lag:
            turn(i - lag, 2)

    def compact(c, segment):
        held = jnp.where(s == segment, 0, 1)

        @pl.loop(0, 4)
        def _(g):
            for j in range(16):
                yy, zz = 2 * g + j // NR, j % NR
                a, b = ((zz, yy), (yy, zz))[segment]
                at_a, at_b = ((z, y), (y, z))[segment]
                block = bufs[c][held, spot(b - at_b), spot(a - at_a), 0:48]
                tmp[45 * j : 45 * j + 48, :] = block.astype(F32)
            w_ref[segment, c, pl.ds(pl.multiple_of(g * 720, 16), 720), :] = tmp[0:720, :].astype(BF16)

    def spot(by):
        by = lax.rem(by + NR, NR)
        return jnp.where(by < 4, 2 * by, 15 - 2 * by)

    def compact_points(segment):
        held = jnp.where(s == segment, 0, 1)

        @pl.loop(0, NR)
        def _(g):
            for k in range(2):
                for j in range(NR):
                    a, b = ((j, g), (g, j))[segment]
                    at_a, at_b = ((z, y), (y, z))[segment]
                    block = buf0[held, spot(b - at_b), spot(a - at_a), 48:64]
                    tmp2[k, 5 * j : 5 * j + 8, :] = block.astype(F32)[8 * k : 8 * k + 8]
                pwf[k, pl.ds(pl.multiple_of(g * 40, 8), 40), :] = tmp2[k, 0:40, :]
        pw_ref[segment] = pwf[...].astype(BF16)

    def store(ref, value):
        ref[1 : ROWS + 1] = value.astype(BF16).reshape(ROWS, WC, C)

    def inner(ref):
        return flat(ref[1 : ROWS + 1])

    def swap(ref, i):
        push(ref.at[s], ref.at[s], e_s.at[i], e_r.at[i], other)

    def swapped(ref, i):
        arrived(ref.at[1 - s], e_s.at[i], e_r.at[i])

    for k in range(1, NX):
        arrived(xin.at[:, pl.ds(4 * row_of(-k) + 1, 4)], i_s.at[k], i_r.at[k])
    lat, hint, dec, tgt = xin.at[0], xin.at[1], xin.at[2], xin.at[3]
    wait_d(0)
    for segment in range(2):
        compact_points(segment)
        compact(0, segment)
    own_in = cin2.at[s]
    store(own_in, mm(inner(hint), pw_ref[0, 0]) + inner(lat).astype(F32))
    swap(cin2, 0)
    pre = conv(own_in, w_ref, 0, 0)
    pre_c[...] = pre
    store(act, silu(pre))
    pre_d[...] = conv(dec, w_ref, 1, 0)
    turn(9, 2)
    wait_d(1)
    for segment in range(2):
        compact(1, segment)
    store(eact, silu(conv(lat, w_ref, 0, 1)))
    turn(10, 2)
    base[...] = conv(eact, w_ref, 1, 1) + inner(lat).astype(F32)
    turn(11, 2)
    wait_d(2)
    for segment in range(2):
        compact(2, segment)
    out = (conv(act, w_ref, 0, 2) + inner(own_in).astype(F32)).astype(BF16)
    co2[s] = out
    swap(co2, 1)
    proj = mm(out, pw_ref[0, 1]).astype(BF16)
    store(skip_p, base[...] + proj.astype(F32))
    pre = pre_d[...] + conv(skip_p, w_ref, 1, 2)
    output = silu(pre) + mm(inner(dec), pw_ref[1, 0]) + mm(inner(skip_p), pw_ref[1, 1])
    error = (output - inner(tgt).astype(F32)) * (1.0 / math.sqrt(128 * ROWS * WC))
    store(dg, error * slope(pre))
    back = conv_back(dg, w_ref, 1, 2) + mm_t(error.astype(BF16), pw_ref[1, 1])
    sg = back.astype(BF16)
    sg2[s] = sg
    swap(sg2, 2)
    store(act, mm_t(sg, pw_ref[0, 1]))
    grad = conv_back(act, w_ref, 0, 2) * slope(pre_c[...])
    fg2[s] = grad.astype(BF16)
    swap(fg2, 3)

    swapped(cin2, 0)
    swapped(co2, 1)
    swapped(sg2, 2)
    for tap in range(5):
        line = jnp.where(zero, tap // 3, (4 + tap) // 3)
        start = jnp.where(zero, FIRST_SLOTS[0][tap], FIRST_SLOTS[1][tap])
        m = lax.broadcasted_iota(jnp.int32, (128, C), 0)
        c = lax.broadcasted_iota(jnp.int32, (128, C), 1)
        row = ((180 * (start + (m >> 3)) + 45 * r) >> 3) + (m & 7) - (C * tap - 160 * s)
        pick = jnp.where((c == row) & ((m & 7) < 7), 1.0, 0.0).astype(BF16)
        held = flat(cin2[:, pl.ds(line, ROWS)])
        xsel[tap] = mm_t(pick, held).astype(BF16)
    m = lax.broadcasted_iota(jnp.int32, (128, C), 0)
    c = lax.broadcasted_iota(jnp.int32, (128, C), 1)
    row = 160 * s + ((20 * (m & 63) + 5 * r) >> 3) + (m >> 6)
    pick = jnp.where(c == row, 1.0, 0.0).astype(BF16)
    picked = mm_t(pick, flat(co2[...])).astype(BF16)
    pair = mm(picked, flat(sg2[...]))
    m = lax.broadcasted_iota(jnp.int32, (64, C), 0)
    lane = lax.broadcasted_iota(jnp.int32, (64, C), 1)
    zs[...] = jnp.where(lane >= 40 * ((4 * m + 5 * r) & 7), pair[0:64], pair[64:128])
    slots[...] = jnp.zeros(slots.shape, F32)
    for i in range(64):
        slots[i, 7:8, :] = zs[i : i + 1, :]

    swapped(fg2, 3)
    whole = flat(fg2[...])
    wide = whole.astype(F32)
    fgs[1] = whole
    fgs[0] = moved(wide, -1).astype(BF16)
    fgs[2] = moved(wide, 1).astype(BF16)
    for tap in range(5):
        column = jnp.where(zero, tap % 3, (4 + tap) % 3)
        start = jnp.where(zero, FIRST_SLOTS[0][tap], FIRST_SLOTS[1][tap])
        slots[pl.ds(start, 16)] += mm(xsel[tap], fgs[column]).reshape(16, NR, C)

    @pl.when(zero)
    def _():
        for a in range(NR):
            rsb[a] = jnp.concatenate([slots[NR * b + a] for b in range(NR)], axis=0).astype(BF16)

    @pl.when(s == 1)
    def _():
        for a in range(NR):
            rsb[a] = jnp.concatenate([slots[NR * a + b] for b in range(NR)], axis=0).astype(BF16)

    for k in range(1, NR):
        push(rsb.at[ring(pa, k)], rsr.at[k], r1_s.at[k], r1_r.at[k], dev(k, 0))
    total = rsb[pa].astype(F32)
    for k in range(1, NR):
        arrived(rsr.at[k], r1_s.at[k], r1_r.at[k])
        total = total + rsr[k].astype(F32)
    s2b[...] = total.reshape(NR, NR, C)
    for k in range(1, NR):
        push(s2b.at[ring(pb, k)], s2r.at[k], r2_s.at[k], r2_r.at[k], dev(0, k))
    total = s2b[pb]
    for k in range(1, NR):
        arrived(s2r.at[k], r2_s.at[k], r2_r.at[k])
        total = total + s2r[k]
    out_ref[...] = total
    for copy in sends:
        copy.wait_send()


def per_device(latent, hint, decoder_in, target, first_convs, second_convs, pointwise):
    pwk = jnp.pad(pointwise[0], ((0, 0), (0, 3), (0, 0))).reshape(16, C)
    vm = pltpu.VMEM
    dma = pltpu.SemaphoreType.DMA
    image = (ROWS + 2, WC, C)
    cells = (CELLS, C)
    scratch = [vm((2, NR, NR, height, C), BF16) for height in HEIGHTS]
    scratch += [
        vm((2, 3, 9 * C, C), BF16), vm((2, 2, C, C), BF16), vm((728, C), F32), vm((2, 48, C), F32), vm((2, C, C), F32),
        vm((4,) + image, BF16), vm((2,) + image, BF16), vm((2,) + cells, BF16), vm((2,) + cells, BF16),
        vm((2,) + cells, BF16), vm(cells, F32), vm(cells, F32), vm(cells, F32),
        vm(image, BF16), vm(image, BF16), vm(image, BF16), vm(image, BF16),
        vm((5, 128, 2 * CELLS), BF16), vm((3, 2 * CELLS, C), BF16), vm((64, C), F32),
        vm((64, NR, C), F32), vm((NR, 64, C), BF16), vm((NR, 64, C), BF16), vm((NR, NR, C), F32), vm((NR, NR, C), F32),
    ]
    for shape in ((3, 2, 4), (3, 2, 2, 4), (3, 2, 4), (3, 5), (4,), (4,), (NR,), (NR,)):
        scratch += [dma(shape), dma(shape)]
    got = pl.pallas_call(
        kernel,
        out_shape=jax.ShapeDtypeStruct((8, C), F32),
        in_specs=[pl.BlockSpec(memory_space=pltpu.VMEM)] * 7,
        out_specs=pl.BlockSpec(memory_space=pltpu.VMEM),
        scratch_shapes=scratch,
        compiler_params=pltpu.CompilerParams(
            collective_id=0, has_side_effects=True, vmem_limit_bytes=60 * 1024 * 1024
        ),
        name="step",
    )(latent, hint, decoder_in, target, first_convs, second_convs, pwk)
    d = lax.axis_index("dp")
    r = lax.axis_index("rows")
    offset = 40 * ((4 * d + 5 * r) & 7)
    first = lax.dynamic_slice(got[:7].reshape(-1), (offset,), (1800,))
    last = got[7]
    second = lax.dynamic_slice(jnp.concatenate([last, last]), (offset,), (200,))
    return first, second


def solution(mesh):
    placed = (
        P("dp", "rows", None, None),
        P("dp", "rows", None, None),
        P("dp", "rows", None, None),
        P("dp", "rows", None, None),
        P("segment", None, "dp", None),
        P("segment", "dp", None),
        P("segment", None, "dp", None),
    )
    return jax.shard_map(
        per_device,
        mesh=mesh,
        in_specs=placed,
        out_specs=(P(("segment", "dp", "rows")), P(("segment", "dp", "rows"))),
        check_vma=False,
    )
```

```python
import math

import jax
import jax.numpy as jnp
from jax import lax
from jax.experimental import pallas as pl
from jax.experimental.pallas import tpu as pltpu
from jax.sharding import PartitionSpec as P

F32 = jnp.float32
BF16 = jnp.bfloat16
C = 320
WC = 16
NX = 4
NR = 8
ROWS = 16
CELLS = ROWS * WC
BLOCKS = ((32, 640), (48, 384), (48, 256))
WIDE = 384
LAGS = (0, 1, 3)
FAR = (4, 3, 5, 2, 6, 1, 7)
ALONE = (2, 2, 2)
FIRST_SLOTS = ((0, 14, 28, 42, 48), (0, 7, 21, 35, 48))
MESH = pl.DeviceIdType.MESH


def slope(value):
    logistic = 1.0 / (1.0 + jnp.exp(-value))
    return logistic * (1.0 + value * (1.0 - logistic))


def silu(value):
    return value / (1.0 + jnp.exp(-value))


def mm(left, right):
    return jnp.dot(left, right, preferred_element_type=F32)


def mm_t(left, right):
    return lax.dot_general(left, right, (((1,), (1,)), ((), ())), preferred_element_type=F32)


def flat(value):
    return value.reshape(-1, value.shape[-1])


def moved(value, by):
    count = value.shape[0]
    column = lax.broadcasted_iota(jnp.int32, value.shape, 0) & (WC - 1)
    rolled = pltpu.roll(value, by % count, 0)
    edge = 0 if by == 1 else WC - 1
    return jnp.where(column == edge, 0.0, rolled)


def taps(load, w_ref, segment, chunk, product):
    parts = []
    for b in range(3):
        total = None
        for a in range(3):
            term = product(load(a), w_ref[segment, chunk, (3 * a + b) * C : (3 * a + b + 1) * C, :])
            total = term if total is None else total + term
        parts.append(total)
    return parts


def conv(ref, w_ref, segment, chunk):
    parts = taps(lambda a: flat(ref[a : a + ROWS]), w_ref, segment, chunk, mm)
    return parts[1] + moved(parts[0], 1) + moved(parts[2], -1)


def conv_back(ref, w_ref, segment, chunk):
    parts = taps(lambda a: flat(ref[2 - a : 2 - a + ROWS]), w_ref, segment, chunk, mm_t)
    return parts[1] + moved(parts[0], -1) + moved(parts[2], 1)


def place(by):
    if by == 0:
        return 0
    return 7 if abs(by) == 4 else 2 * by if by > 0 else -2 * by - 1


def kernel(
    lat_ref, hint_ref, dec_ref, tgt_ref, first_ref, second_ref, points_ref, out_ref,
    buf0, buf1, buf2, w_ref, pw_ref, tmp, tmp2, pwf,
    pack, xin, cin2, co2, sg2, fg2, pre_c, pre_d, base, act, eact, skip_p, dg, xsel, fgs, zs,
    slots, rsb, rsr, s2b, s2r,
    a_s, a_r, b_s, b_r, x_s, x_r, d_s, d_r, i_s, i_r, e_s, e_r, r1_s, r1_r, r2_s, r2_r, l_s,
):
    s = lax.axis_index("segment")
    d = lax.axis_index("dp")
    r = lax.axis_index("rows")
    zero = s == 0
    y = d // NR
    z = lax.rem(d, NR)
    pa = jnp.where(zero, z, y)
    pb = jnp.where(zero, y, z)
    odd = lax.rem(r, 2)
    own = 4 * r
    bufs = (buf0, buf1, buf2)

    def ring(position, by):
        return lax.rem(position + by + NR, NR)

    def dev(by_a, by_b):
        a, b = ring(pa, by_a), ring(pb, by_b)
        return (s, jnp.where(zero, b * NR + a, a * NR + b), r)

    def row_of(k):
        return lax.rem(r + k + NX, NX)

    other = (1 - s, d, r)
    sends = []

    def rcopy(src, dst, send, recv, device):
        return pltpu.make_async_remote_copy(
            src_ref=src, dst_ref=dst, send_sem=send, recv_sem=recv,
            device_id=device, device_id_type=MESH,
        )

    def push(src, dst, send, recv, device):
        copy = rcopy(src, dst, send, recv, device)
        copy.start()
        sends.append(copy)

    def arrived(dst, send, recv):
        rcopy(dst, dst, send, recv, other).wait_recv()

    inputs = [
        pltpu.make_async_copy(ref.at[s], xin.at[i, pl.ds(own + 1, 4)], l_s.at[i])
        for i, ref in enumerate((lat_ref, hint_ref, dec_ref, tgt_ref))
    ]

    def joined(left, right):
        lane = lax.broadcasted_iota(jnp.int32, (left.shape[0], 128), 1)
        return jnp.where(lane < 64, left[:, 256:384], pltpu.roll(right[:, 256:384], 64, 1)).astype(BF16)

    for copy in inputs:
        copy.start()
    pack[...] = jnp.zeros(pack.shape, F32)
    pack[0, 0:45, 0:C] = first_ref[:, 1, :].astype(F32)
    pack[1, 0:45, 0:C] = first_ref[:, 0, :].astype(F32)
    pack[2, 0:45, 0:C] = second_ref[0].astype(F32)
    pack[0, 48:53, 0:C] = points_ref[:, 0, :].astype(F32)
    pack[0, 56:61, 0:C] = points_ref[:, 1, :].astype(F32)
    low, high = pack[0, 0:32], pack[0, 32:64]
    buf0[0, 0, 0, :, 0:256] = low[:, 0:256].astype(BF16)
    buf0[0, 0, 0, :, 256:512] = high[:, 0:256].astype(BF16)
    buf0[0, 0, 0, :, 512:640] = joined(low, high)
    buf1[0, 0, 0, :, 0:256] = pack[1, 0:48, 0:256].astype(BF16)
    buf1[0, 0, 0, :, 256:384] = joined(pack[1, 0:48], pack[2, 0:48])
    buf2[0, 0, 0] = pack[2, 0:48, 0:256].astype(BF16)
    edge = jnp.zeros((1, WC, C), BF16)
    for ref in [xin.at[0], xin.at[2], cin2.at[0], cin2.at[1], act, eact, skip_p, dg]:
        ref[0:1] = edge
        ref[ROWS + 1 : ROWS + 2] = edge
    barrier = pltpu.get_barrier_semaphore()
    peers = [dev(k, 0) for k in range(1, NR)] + [dev(0, k) for k in range(1, NR)]
    peers += [(s, d, row_of(k)) for k in range(1, NX)] + [other]
    for peer in peers:
        pl.semaphore_signal(barrier, inc=1, device_id=peer, device_id_type=MESH)
    pl.semaphore_wait(barrier, len(peers))

    def a_part(c, k, way):
        return bufs[c].at[0, 0, place(k if way else -k)]

    def send_a(c, k):
        for way in range(2 if k < 4 else 1):
            push(a_part(c, k - 1, way), a_part(c, k, way), a_s.at[c, way, k - 1], a_r.at[c, way, k - 1], dev(-1 if way else 1, 0))

    def wait_a(c, k):
        for way in range(2 if k < 4 else 1):
            arrived(a_part(c, k, way), a_s.at[c, way, k - 1], a_r.at[c, way, k - 1])

    def mine(c):
        return pl.ds(ALONE[c] * odd, ALONE[c])

    def theirs(c):
        return pl.ds(ALONE[c] * (1 - odd), ALONE[c])

    def both(c):
        return pl.ds(2 * ALONE[c], NR - 2 * ALONE[c])

    def ways(part, k):
        return (0, 1) if k < 4 else (part,)

    def b_part(c, part, k, way):
        which = mine(c) if part else both(c)
        return bufs[c].at[0, place(k if way else -k), which]

    def send_b(c, part, k):
        for way in ways(part, k):
            push(
                b_part(c, part, k - 1, way), b_part(c, part, k, way),
                b_s.at[c, part, way, k - 1], b_r.at[c, part, way, k - 1], dev(0, -1 if way else 1),
            )

    def wait_b(c, part, k):
        for way in ways(part, k):
            arrived(b_part(c, part, k, way), b_s.at[c, part, way, k - 1], b_r.at[c, part, way, k - 1])

    def send_x(c, k):
        for way in ways(1, k):
            ref = b_part(c, 1, k, way)
            push(ref, ref, x_s.at[c, way, k - 1], x_r.at[c, way, k - 1], (s, d, row_of(-1 if way else 1)))

    def wait_x(c, k):
        for way in ways(1, k):
            ref = bufs[c].at[0, place(k if way else -k), theirs(c)]
            arrived(ref, x_s.at[c, way, k - 1], x_r.at[c, way, k - 1])

    def span(k):
        return pl.ds(0, 1) if k == 0 else pl.ds(7, 1) if k == 4 else pl.ds(2 * k - 1, 2)

    def send_d(c, k):
        push(bufs[c].at[0, span(k)], bufs[c].at[1, span(k)], d_s.at[c, k], d_r.at[c, k], other)

    def wait_d(c):
        for k in range(5):
            arrived(bufs[c].at[1, span(k)], d_s.at[c, k], d_r.at[c, k])

    def turn(i, c):
        if i == 0:
            send_a(c, 1)
        elif i == 1:
            wait_a(c, 1)
            send_a(c, 2)
        elif i == 2:
            wait_a(c, 2)
            send_a(c, 3)
            send_b(c, 1, 1)
        elif i == 3:
            wait_a(c, 3)
            send_a(c, 4)
            wait_b(c, 1, 1)
            send_b(c, 1, 2)
            send_x(c, 1)
        elif i == 4:
            wait_a(c, 4)
            send_b(c, 0, 1)
            send_d(c, 0)
        elif i in (5, 7, 9):
            k = (i - 1) // 2
            wait_b(c, 1, k)
            if k < 4:
                send_b(c, 1, k + 1)
            send_x(c, k)
            if i > 5:
                send_xd(c, k - 2)
        elif i in (6, 8, 10):
            k = (i - 4) // 2
            wait_b(c, 0, k)
            send_b(c, 0, k + 1)
        elif i == 11:
            send_xd(c, 3)
            wait_b(c, 0, 4)
            send_xd(c, 4)

    def send_xd(c, k):
        wait_x(c, k)
        send_d(c, k)

    for c in range(3):
        turn(0, c)
    for copy in inputs:
        copy.wait()

    def rows_of(k, half=None):
        which = pl.ds(0, 4) if half is None else pl.ds(2 * half, 2)
        return xin.at[which, pl.ds(4 * row_of(k) + 1, 4)]

    for i, k in enumerate((1, -1)):
        push(rows_of(0), rows_of(0), i_s.at[0, i], i_r.at[0, i], (s, d, row_of(k)))
    for i in range(1, 12):
        turn(i, 0)
        for c in (1, 2):
            if i < 4:
                turn(i, c)
            elif i - LAGS[c] > 3:
                turn(i - LAGS[c], c)
        if i == 3:
            for at, k in enumerate((1, -1)):
                arrived(rows_of(-k), i_s.at[0, at], i_r.at[0, at])
                ref = rows_of(-k, at)
                push(ref, ref, i_s.at[1, at], i_r.at[1, at], (s, d, row_of(k)))

    def spot(by):
        by = lax.rem(by + NR, NR)
        return jnp.where(by < 4, 2 * by, 15 - 2 * by)

    def spots(segment, yy, zz):
        first = segment == 0
        at_y, at_z = spot(yy - y), spot(zz - z)
        return jnp.where(first, at_y, at_z), jnp.where(first, at_z, at_y)

    def tail(block):
        return pltpu.roll(block, 64, 1)[:, 0:64]

    def compact(c, held):
        segment = jnp.where(held == 0, s, 1 - s)

        @pl.loop(0, 4)
        def _(g):
            for j in range(16):
                at = (held,) + spots(segment, 2 * g + j // NR, j % NR)
                row = 45 * j
                if c == 0:
                    low, high = buf0[at], buf0[at + (slice(0, 16),)]
                    tmp[row : row + 32, 0:256] = low[:, 0:256].astype(F32)
                    tmp[row : row + 32, 256:C] = low[:, 512:576].astype(F32)
                    tmp[row + 32 : row + 48, 0:256] = high[:, 256:512].astype(F32)
                    tmp[row + 32 : row + 48, 256:C] = tail(high[:, 512:640].astype(F32))
                elif c == 1:
                    tmp[row : row + 48, :] = buf1[at][:, 0:C].astype(F32)
                else:
                    tmp[row : row + 48, 0:256] = buf2[at].astype(F32)
                    tmp[row : row + 48, 256:C] = tail(buf1[at][:, 256:384].astype(F32))
            w_ref[segment, c, pl.ds(pl.multiple_of(g * 720, 16), 720), :] = tmp[0:720, :].astype(BF16)

    def compact_points(held):
        segment = jnp.where(held == 0, s, 1 - s)

        @pl.loop(0, NR)
        def _(g):
            for j in range(NR):
                block = buf0[(held,) + spots(segment, g, j) + (slice(16, 32),)]
                main, last = block[:, 256:512].astype(F32), tail(block[:, 512:640].astype(F32))
                for k in range(2):
                    tmp2[k, 5 * j : 5 * j + 8, 0:256] = main[8 * k : 8 * k + 8]
                    tmp2[k, 5 * j : 5 * j + 8, 256:C] = last[8 * k : 8 * k + 8]
            for k in range(2):
                pwf[k, pl.ds(pl.multiple_of(g * 40, 8), 40), :] = tmp2[k, 0:40, :]
        pw_ref[segment] = pwf[...].astype(BF16)

    def store(ref, value):
        ref[1 : ROWS + 1] = value.astype(BF16).reshape(ROWS, WC, C)

    def inner(ref):
        return flat(ref[1 : ROWS + 1])

    def swap(ref, i):
        push(ref.at[s], ref.at[s], e_s.at[i], e_r.at[i], other)

    def swapped(ref, i):
        arrived(ref.at[1 - s], e_s.at[i], e_r.at[i])

    for i in range(2):
        arrived(rows_of(2, i), i_s.at[1, i], i_r.at[1, i])
    lat, hint, dec, tgt = xin.at[0], xin.at[1], xin.at[2], xin.at[3]
    compact_points(0)
    compact(0, 0)
    turn(11, 1)
    turn(9, 2)
    wait_d(0)
    compact_points(1)
    compact(0, 1)
    turn(10, 2)
    own_in = cin2.at[s]
    store(own_in, mm(inner(hint), pw_ref[0, 0]) + inner(lat).astype(F32))
    swap(cin2, 0)
    pre = conv(own_in, w_ref, 0, 0)
    pre_c[...] = pre
    store(act, silu(pre))
    compact(1, 0)
    pre_d[...] = conv(dec, w_ref, 1, 0)
    turn(11, 2)
    wait_d(1)
    compact(1, 1)
    store(eact, silu(conv(lat, w_ref, 0, 1)))
    base[...] = conv(eact, w_ref, 1, 1) + inner(lat).astype(F32)
    compact(2, 0)
    swapped(cin2, 0)
    for tap in range(5):
        line = jnp.where(zero, tap // 3, (4 + tap) // 3)
        start = jnp.where(zero, FIRST_SLOTS[0][tap], FIRST_SLOTS[1][tap])
        m = lax.broadcasted_iota(jnp.int32, (128, C), 0)
        c = lax.broadcasted_iota(jnp.int32, (128, C), 1)
        row = ((180 * (start + (m >> 3)) + 45 * r) >> 3) + (m & 7) - (C * tap - 160 * s)
        pick = jnp.where((c == row) & ((m & 7) < 7), 1.0, 0.0).astype(BF16)
        held = flat(cin2[:, pl.ds(line, ROWS)])
        xsel[tap] = mm_t(pick, held).astype(BF16)
    wait_d(2)
    compact(2, 1)
    out = (conv(act, w_ref, 0, 2) + inner(own_in).astype(F32)).astype(BF16)
    co2[s] = out
    swap(co2, 1)
    proj = mm(out, pw_ref[0, 1]).astype(BF16)
    store(skip_p, base[...] + proj.astype(F32))
    pre = pre_d[...] + conv(skip_p, w_ref, 1, 2)
    output = silu(pre) + mm(inner(dec), pw_ref[1, 0]) + mm(inner(skip_p), pw_ref[1, 1])
    error = (output - inner(tgt).astype(F32)) * (1.0 / math.sqrt(128 * ROWS * WC))
    store(dg, error * slope(pre))
    back = conv_back(dg, w_ref, 1, 2) + mm_t(error.astype(BF16), pw_ref[1, 1])
    sg = back.astype(BF16)
    sg2[s] = sg
    swap(sg2, 2)
    store(act, mm_t(sg, pw_ref[0, 1]))
    grad = conv_back(act, w_ref, 0, 2) * slope(pre_c[...])
    fg2[s] = grad.astype(BF16)
    swap(fg2, 3)

    swapped(co2, 1)
    swapped(sg2, 2)
    m = lax.broadcasted_iota(jnp.int32, (128, C), 0)
    c = lax.broadcasted_iota(jnp.int32, (128, C), 1)
    row = 160 * s + ((20 * (m & 63) + 5 * r) >> 3) + (m >> 6)
    pick = jnp.where(c == row, 1.0, 0.0).astype(BF16)
    picked = mm_t(pick, flat(co2[...])).astype(BF16)
    pair = mm(picked, flat(sg2[...]))
    m = lax.broadcasted_iota(jnp.int32, (64, C), 0)
    lane = lax.broadcasted_iota(jnp.int32, (64, C), 1)
    zs[...] = jnp.where(lane >= 40 * ((4 * m + 5 * r) & 7), pair[0:64], pair[64:128])
    slots[...] = jnp.zeros(slots.shape, F32)
    for i in range(64):
        slots[i, 7:8, :] = zs[i : i + 1, :]

    swapped(fg2, 3)
    whole = flat(fg2[...])
    wide = whole.astype(F32)
    fgs[1] = whole
    fgs[0] = moved(wide, -1).astype(BF16)
    fgs[2] = moved(wide, 1).astype(BF16)
    for tap in range(5):
        column = jnp.where(zero, tap % 3, (4 + tap) % 3)
        start = jnp.where(zero, FIRST_SLOTS[0][tap], FIRST_SLOTS[1][tap])
        slots[pl.ds(start, 16)] += mm(xsel[tap], fgs[column]).reshape(16, NR, C)

    @pl.when(zero)
    def _():
        for a in range(NR):
            rsb[a] = jnp.concatenate([slots[NR * b + a] for b in range(NR)], axis=0).astype(BF16)

    @pl.when(s == 1)
    def _():
        for a in range(NR):
            rsb[a] = jnp.concatenate([slots[NR * a + b] for b in range(NR)], axis=0).astype(BF16)

    for k in FAR:
        push(rsb.at[ring(pa, k)], rsr.at[k], r1_s.at[k], r1_r.at[k], dev(k, 0))
    total = rsb[pa].astype(F32)
    for k in range(1, NR):
        arrived(rsr.at[k], r1_s.at[k], r1_r.at[k])
        total = total + rsr[k].astype(F32)
    s2b[...] = total.reshape(NR, NR, C)
    for k in FAR:
        push(s2b.at[ring(pb, k)], s2r.at[k], r2_s.at[k], r2_r.at[k], dev(0, k))
    total = s2b[pb]
    for k in range(1, NR):
        arrived(s2r.at[k], r2_s.at[k], r2_r.at[k])
        total = total + s2r[k]
    off = 40 * ((4 * d + 5 * r) & 7)
    wide = jnp.concatenate([total, jnp.zeros((NR, WIDE - C), F32)], axis=1)
    after = jnp.where(lax.broadcasted_iota(jnp.int32, wide.shape, 0) == 7, wide, pltpu.roll(wide, 7, 0))
    lane = lax.broadcasted_iota(jnp.int32, wide.shape, 1)
    wide = jnp.where(lane < C - off, pltpu.roll(wide, lax.rem(WIDE - off, WIDE), 1), pltpu.roll(after, C - off, 1))
    out_ref[...] = wide[:, 0:C]
    for copy in sends:
        copy.wait_send()


def per_device(latent, hint, decoder_in, target, first_convs, second_convs, pointwise):
    vm = pltpu.VMEM
    dma = pltpu.SemaphoreType.DMA
    image = (ROWS + 2, WC, C)
    cells = (CELLS, C)
    scratch = [vm((2, NR, NR) + block, BF16) for block in BLOCKS]
    scratch += [
        vm((2, 3, 9 * C, C), BF16), vm((2, 2, C, C), BF16), vm((728, C), F32), vm((2, 48, C), F32), vm((2, C, C), F32),
        vm((3, 64, WIDE), F32), vm((4,) + image, BF16), vm((2,) + image, BF16), vm((2,) + cells, BF16), vm((2,) + cells, BF16),
        vm((2,) + cells, BF16), vm(cells, F32), vm(cells, F32), vm(cells, F32),
        vm(image, BF16), vm(image, BF16), vm(image, BF16), vm(image, BF16),
        vm((5, 128, 2 * CELLS), BF16), vm((3, 2 * CELLS, C), BF16), vm((64, C), F32),
        vm((64, NR, C), F32), vm((NR, 64, C), BF16), vm((NR, 64, C), BF16), vm((NR, NR, C), F32), vm((NR, NR, C), F32),
    ]
    for shape in ((3, 2, 4), (3, 2, 2, 4), (3, 2, 4), (3, 5), (2, 2), (4,), (NR,), (NR,)):
        scratch += [dma(shape), dma(shape)]
    scratch += [dma((4,))]
    got = pl.pallas_call(
        kernel,
        out_shape=jax.ShapeDtypeStruct((8, C), F32),
        in_specs=[pl.BlockSpec(memory_space=pl.ANY)] * 4 + [pl.BlockSpec(memory_space=pltpu.VMEM)] * 3,
        out_specs=pl.BlockSpec(memory_space=pltpu.VMEM),
        scratch_shapes=scratch,
        compiler_params=pltpu.CompilerParams(
            collective_id=0, has_side_effects=True, vmem_limit_bytes=60 * 1024 * 1024
        ),
        name="step",
    )(latent, hint, decoder_in, target, jnp.swapaxes(first_convs[0], 0, 1), second_convs, jnp.swapaxes(pointwise[0], 0, 1))
    return got[:6].reshape(-1)[:1800], got[7, :200]


def solution(mesh):
    placed = (
        P("dp", "rows", None, None),
        P("dp", "rows", None, None),
        P("dp", "rows", None, None),
        P("dp", "rows", None, None),
        P("segment", None, "dp", None),
        P("segment", "dp", None),
        P("segment", None, "dp", None),
    )
    return jax.shard_map(
        per_device,
        mesh=mesh,
        in_specs=placed,
        out_specs=(P(("segment", "dp", "rows")), P(("segment", "dp", "rows"))),
        check_vma=False,
    )
```

```python
import math

import jax
import jax.numpy as jnp
from jax import lax
from jax.experimental import pallas as pl
from jax.experimental.pallas import tpu as pltpu
from jax.sharding import PartitionSpec as P

F32 = jnp.float32
BF16 = jnp.bfloat16
C = 320
WC = 16
NX = 4
NR = 8
ROWS = 16
CELLS = ROWS * WC
BLOCKS = ((32, 640), (48, 384), (48, 256))
WIDE = 384
LAGS = (0, 1, 3)
FAR = (4, 3, 5, 2, 6, 1, 7)
ALONE = (2, 2, 2)
FIRST_SLOTS = ((0, 14, 28, 42, 48), (0, 7, 21, 35, 48))
MESH = pl.DeviceIdType.MESH


def slope(value):
    logistic = 1.0 / (1.0 + jnp.exp(-value))
    return logistic * (1.0 + value * (1.0 - logistic))


def silu(value):
    return value / (1.0 + jnp.exp(-value))


def mm(left, right):
    return jnp.dot(left, right, preferred_element_type=F32)


def mm_t(left, right):
    return lax.dot_general(left, right, (((1,), (1,)), ((), ())), preferred_element_type=F32)


def flat(value):
    return value.reshape(-1, value.shape[-1])


def moved(value, by):
    count = value.shape[0]
    column = lax.broadcasted_iota(jnp.int32, value.shape, 0) & (WC - 1)
    rolled = pltpu.roll(value, by % count, 0)
    edge = 0 if by == 1 else WC - 1
    return jnp.where(column == edge, 0.0, rolled)


def taps(load, w_ref, segment, chunk, product):
    parts = []
    for b in range(3):
        total = None
        for a in range(3):
            term = product(load(a), w_ref[segment, chunk, (3 * a + b) * C : (3 * a + b + 1) * C, :])
            total = term if total is None else total + term
        parts.append(total)
    return parts


def conv(ref, w_ref, segment, chunk):
    parts = taps(lambda a: flat(ref[a : a + ROWS]), w_ref, segment, chunk, mm)
    return parts[1] + moved(parts[0], 1) + moved(parts[2], -1)


def conv_back(ref, w_ref, segment, chunk):
    parts = taps(lambda a: flat(ref[2 - a : 2 - a + ROWS]), w_ref, segment, chunk, mm_t)
    return parts[1] + moved(parts[0], -1) + moved(parts[2], 1)


def place(by):
    if by == 0:
        return 0
    return 7 if abs(by) == 4 else 2 * by if by > 0 else -2 * by - 1


def kernel(
    lat_ref, hint_ref, dec_ref, tgt_ref, first_ref, second_ref, points_ref, out_ref,
    buf0, buf1, buf2, w_ref, pw_ref, tmp, tmp2, pwf,
    pack, xin, cin2, co2, sg2, fg2, pre_c, pre_d, base, act, eact, skip_p, dg, xsel, fgs, zs,
    slots, rsb, rsr, s2b, s2r,
    a_s, a_r, b_s, b_r, x_s, x_r, d_s, d_r, i_s, i_r, e_s, e_r, r1_s, r1_r, r2_s, r2_r, l_s,
):
    s = lax.axis_index("segment")
    d = lax.axis_index("dp")
    r = lax.axis_index("rows")
    zero = s == 0
    y = d // NR
    z = lax.rem(d, NR)
    pa = jnp.where(zero, z, y)
    pb = jnp.where(zero, y, z)
    odd = lax.rem(r, 2)
    own = 4 * r
    bufs = (buf0, buf1, buf2)

    def ring(position, by):
        return lax.rem(position + by + NR, NR)

    def dev(by_a, by_b):
        a, b = ring(pa, by_a), ring(pb, by_b)
        return (s, jnp.where(zero, b * NR + a, a * NR + b), r)

    def row_of(k):
        return lax.rem(r + k + NX, NX)

    other = (1 - s, d, r)
    sends = []

    def rcopy(src, dst, send, recv, device):
        return pltpu.make_async_remote_copy(
            src_ref=src, dst_ref=dst, send_sem=send, recv_sem=recv,
            device_id=device, device_id_type=MESH,
        )

    def push(src, dst, send, recv, device):
        copy = rcopy(src, dst, send, recv, device)
        copy.start()
        sends.append(copy)

    def arrived(dst, send, recv):
        rcopy(dst, dst, send, recv, other).wait_recv()

    inputs = [
        pltpu.make_async_copy(ref.at[s], xin.at[i, pl.ds(own + 1, 4)], l_s.at[i])
        for i, ref in enumerate((lat_ref, hint_ref, dec_ref, tgt_ref))
    ]

    def joined(left, right):
        lane = lax.broadcasted_iota(jnp.int32, (left.shape[0], 128), 1)
        return jnp.where(lane < 64, left[:, 256:384], pltpu.roll(right[:, 256:384], 64, 1)).astype(BF16)

    for copy in inputs:
        copy.start()
    pack[...] = jnp.zeros(pack.shape, F32)
    pack[0, 0:45, 0:C] = first_ref[:, 1, :].astype(F32)
    pack[1, 0:45, 0:C] = first_ref[:, 0, :].astype(F32)
    pack[2, 0:45, 0:C] = second_ref[0].astype(F32)
    pack[0, 48:53, 0:C] = points_ref[:, 0, :].astype(F32)
    pack[0, 56:61, 0:C] = points_ref[:, 1, :].astype(F32)
    low, high = pack[0, 0:32], pack[0, 32:64]
    buf0[0, 0, 0, :, 0:256] = low[:, 0:256].astype(BF16)
    buf0[0, 0, 0, :, 256:512] = high[:, 0:256].astype(BF16)
    buf0[0, 0, 0, :, 512:640] = joined(low, high)
    buf1[0, 0, 0, :, 0:256] = pack[1, 0:48, 0:256].astype(BF16)
    buf1[0, 0, 0, :, 256:384] = joined(pack[1, 0:48], pack[2, 0:48])
    buf2[0, 0, 0] = pack[2, 0:48, 0:256].astype(BF16)
    edge = jnp.zeros((1, WC, C), BF16)
    for ref in [xin.at[0], xin.at[2], cin2.at[0], cin2.at[1], act, eact, skip_p, dg]:
        ref[0:1] = edge
        ref[ROWS + 1 : ROWS + 2] = edge
    barrier = pltpu.get_barrier_semaphore()
    peers = [dev(1, 0), dev(-1, 0), dev(0, 1), dev(0, -1), (s, d, row_of(1)), (s, d, row_of(-1)), other]
    for peer in peers:
        pl.semaphore_signal(barrier, inc=1, device_id=peer, device_id_type=MESH)
    pl.semaphore_wait(barrier, len(peers))

    def a_part(c, k, way):
        return bufs[c].at[0, 0, place(k if way else -k)]

    def send_a(c, k):
        for way in range(2 if k < 4 else 1):
            push(a_part(c, k - 1, way), a_part(c, k, way), a_s.at[c, way, k - 1], a_r.at[c, way, k - 1], dev(-1 if way else 1, 0))

    def wait_a(c, k):
        for way in range(2 if k < 4 else 1):
            arrived(a_part(c, k, way), a_s.at[c, way, k - 1], a_r.at[c, way, k - 1])

    def mine(c):
        return pl.ds(ALONE[c] * odd, ALONE[c])

    def theirs(c):
        return pl.ds(ALONE[c] * (1 - odd), ALONE[c])

    def both(c):
        return pl.ds(2 * ALONE[c], NR - 2 * ALONE[c])

    def ways(part, k):
        return (0, 1) if k < 4 else (part,)

    def b_part(c, part, k, way):
        which = mine(c) if part else both(c)
        return bufs[c].at[0, place(k if way else -k), which]

    def send_b(c, part, k):
        for way in ways(part, k):
            push(
                b_part(c, part, k - 1, way), b_part(c, part, k, way),
                b_s.at[c, part, way, k - 1], b_r.at[c, part, way, k - 1], dev(0, -1 if way else 1),
            )

    def wait_b(c, part, k):
        for way in ways(part, k):
            arrived(b_part(c, part, k, way), b_s.at[c, part, way, k - 1], b_r.at[c, part, way, k - 1])

    def send_x(c, k):
        for way in ways(1, k):
            ref = b_part(c, 1, k, way)
            push(ref, ref, x_s.at[c, way, k - 1], x_r.at[c, way, k - 1], (s, d, row_of(-1 if way else 1)))

    def wait_x(c, k):
        for way in ways(1, k):
            ref = bufs[c].at[0, place(k if way else -k), theirs(c)]
            arrived(ref, x_s.at[c, way, k - 1], x_r.at[c, way, k - 1])

    def span(k):
        return pl.ds(0, 1) if k == 0 else pl.ds(7, 1) if k == 4 else pl.ds(2 * k - 1, 2)

    def send_d(c, k):
        push(bufs[c].at[0, span(k)], bufs[c].at[1, span(k)], d_s.at[c, k], d_r.at[c, k], other)

    def wait_d(c):
        for k in range(5):
            arrived(bufs[c].at[1, span(k)], d_s.at[c, k], d_r.at[c, k])

    def turn(i, c):
        if i == 0:
            send_a(c, 1)
        elif i == 1:
            wait_a(c, 1)
            send_a(c, 2)
        elif i == 2:
            wait_a(c, 2)
            send_a(c, 3)
            send_b(c, 1, 1)
        elif i == 3:
            wait_a(c, 3)
            send_a(c, 4)
            wait_b(c, 1, 1)
            send_b(c, 1, 2)
            send_x(c, 1)
        elif i == 4:
            wait_a(c, 4)
            send_b(c, 0, 1)
            send_d(c, 0)
        elif i in (5, 7, 9):
            k = (i - 1) // 2
            wait_b(c, 1, k)
            if k < 4:
                send_b(c, 1, k + 1)
            send_x(c, k)
            if i > 5:
                send_xd(c, k - 2)
        elif i in (6, 8, 10):
            k = (i - 4) // 2
            wait_b(c, 0, k)
            send_b(c, 0, k + 1)
        elif i == 11:
            send_xd(c, 3)
            wait_b(c, 0, 4)
            send_xd(c, 4)

    def send_xd(c, k):
        wait_x(c, k)
        send_d(c, k)

    for c in range(3):
        turn(0, c)
    for copy in inputs:
        copy.wait()

    def rows_of(k, half=None):
        which = pl.ds(0, 4) if half is None else pl.ds(2 * half, 2)
        return xin.at[which, pl.ds(4 * row_of(k) + 1, 4)]

    for i, k in enumerate((1, -1)):
        push(rows_of(0), rows_of(0), i_s.at[0, i], i_r.at[0, i], (s, d, row_of(k)))
    for i in range(1, 12):
        turn(i, 0)
        for c in (1, 2):
            if i < 4:
                turn(i, c)
            elif i - LAGS[c] > 3:
                turn(i - LAGS[c], c)
        if i == 3:
            for at, k in enumerate((1, -1)):
                arrived(rows_of(-k), i_s.at[0, at], i_r.at[0, at])
                ref = rows_of(-k, at)
                push(ref, ref, i_s.at[1, at], i_r.at[1, at], (s, d, row_of(k)))

    def spot(by):
        by = lax.rem(by + NR, NR)
        return jnp.where(by < 4, 2 * by, 15 - 2 * by)

    def spots(segment, yy, zz):
        first = segment == 0
        at_y, at_z = spot(yy - y), spot(zz - z)
        return jnp.where(first, at_y, at_z), jnp.where(first, at_z, at_y)

    def tail(block):
        return pltpu.roll(block, 64, 1)[:, 0:64]

    def compact(c, held):
        segment = jnp.where(held == 0, s, 1 - s)

        @pl.loop(0, 4)
        def _(g):
            for j in range(16):
                at = (held,) + spots(segment, 2 * g + j // NR, j % NR)
                row = 45 * j
                if c == 0:
                    low, high = buf0[at], buf0[at + (slice(0, 16),)]
                    tmp[row : row + 32, 0:256] = low[:, 0:256].astype(F32)
                    tmp[row : row + 32, 256:C] = low[:, 512:576].astype(F32)
                    tmp[row + 32 : row + 48, 0:256] = high[:, 256:512].astype(F32)
                    tmp[row + 32 : row + 48, 256:C] = tail(high[:, 512:640].astype(F32))
                elif c == 1:
                    tmp[row : row + 48, :] = buf1[at][:, 0:C].astype(F32)
                else:
                    tmp[row : row + 48, 0:256] = buf2[at].astype(F32)
                    tmp[row : row + 48, 256:C] = tail(buf1[at][:, 256:384].astype(F32))
            w_ref[segment, c, pl.ds(pl.multiple_of(g * 720, 16), 720), :] = tmp[0:720, :].astype(BF16)

    def compact_points(held):
        segment = jnp.where(held == 0, s, 1 - s)

        @pl.loop(0, NR)
        def _(g):
            for j in range(NR):
                block = buf0[(held,) + spots(segment, g, j) + (slice(16, 32),)]
                main, last = block[:, 256:512].astype(F32), tail(block[:, 512:640].astype(F32))
                for k in range(2):
                    tmp2[k, 5 * j : 5 * j + 8, 0:256] = main[8 * k : 8 * k + 8]
                    tmp2[k, 5 * j : 5 * j + 8, 256:C] = last[8 * k : 8 * k + 8]
            for k in range(2):
                pwf[k, pl.ds(pl.multiple_of(g * 40, 8), 40), :] = tmp2[k, 0:40, :]
        pw_ref[segment] = pwf[...].astype(BF16)

    def store(ref, value):
        ref[1 : ROWS + 1] = value.astype(BF16).reshape(ROWS, WC, C)

    def inner(ref):
        return flat(ref[1 : ROWS + 1])

    def swap(ref, i):
        push(ref.at[s], ref.at[s], e_s.at[i], e_r.at[i], other)

    def swapped(ref, i):
        arrived(ref.at[1 - s], e_s.at[i], e_r.at[i])

    for i in range(2):
        arrived(rows_of(2, i), i_s.at[1, i], i_r.at[1, i])
    lat, hint, dec, tgt = xin.at[0], xin.at[1], xin.at[2], xin.at[3]
    compact_points(0)
    compact(0, 0)
    turn(9, 2)
    wait_d(0)
    compact_points(1)
    compact(0, 1)
    turn(11, 1)
    turn(10, 2)
    own_in = cin2.at[s]
    store(own_in, mm(inner(hint), pw_ref[0, 0]) + inner(lat).astype(F32))
    swap(cin2, 0)
    pre = conv(own_in, w_ref, 0, 0)
    pre_c[...] = pre
    store(act, silu(pre))
    compact(1, 0)
    pre_d[...] = conv(dec, w_ref, 1, 0)
    turn(11, 2)
    wait_d(1)
    compact(1, 1)
    store(eact, silu(conv(lat, w_ref, 0, 1)))
    base[...] = conv(eact, w_ref, 1, 1) + inner(lat).astype(F32)
    compact(2, 0)
    swapped(cin2, 0)
    for tap in range(5):
        line = jnp.where(zero, tap // 3, (4 + tap) // 3)
        start = jnp.where(zero, FIRST_SLOTS[0][tap], FIRST_SLOTS[1][tap])
        m = lax.broadcasted_iota(jnp.int32, (128, C), 0)
        c = lax.broadcasted_iota(jnp.int32, (128, C), 1)
        row = ((180 * (start + (m >> 3)) + 45 * r) >> 3) + (m & 7) - (C * tap - 160 * s)
        pick = jnp.where((c == row) & ((m & 7) < 7), 1.0, 0.0).astype(BF16)
        held = flat(cin2[:, pl.ds(line, ROWS)])
        xsel[tap] = mm_t(pick, held).astype(BF16)
    wait_d(2)
    compact(2, 1)
    out = (conv(act, w_ref, 0, 2) + inner(own_in).astype(F32)).astype(BF16)
    co2[s] = out
    swap(co2, 1)
    proj = mm(out, pw_ref[0, 1]).astype(BF16)
    store(skip_p, base[...] + proj.astype(F32))
    pre = pre_d[...] + conv(skip_p, w_ref, 1, 2)
    output = silu(pre) + mm(inner(dec), pw_ref[1, 0]) + mm(inner(skip_p), pw_ref[1, 1])
    error = (output - inner(tgt).astype(F32)) * (1.0 / math.sqrt(128 * ROWS * WC))
    store(dg, error * slope(pre))
    back = conv_back(dg, w_ref, 1, 2) + mm_t(error.astype(BF16), pw_ref[1, 1])
    sg = back.astype(BF16)
    sg2[s] = sg
    swap(sg2, 2)
    store(act, mm_t(sg, pw_ref[0, 1]))
    grad = conv_back(act, w_ref, 0, 2) * slope(pre_c[...])
    fg2[s] = grad.astype(BF16)
    swap(fg2, 3)

    swapped(co2, 1)
    swapped(sg2, 2)
    m = lax.broadcasted_iota(jnp.int32, (128, C), 0)
    c = lax.broadcasted_iota(jnp.int32, (128, C), 1)
    row = 160 * s + ((20 * (m & 63) + 5 * r) >> 3) + (m >> 6)
    pick = jnp.where(c == row, 1.0, 0.0).astype(BF16)
    picked = mm_t(pick, flat(co2[...])).astype(BF16)
    pair = mm(picked, flat(sg2[...]))
    m = lax.broadcasted_iota(jnp.int32, (64, C), 0)
    lane = lax.broadcasted_iota(jnp.int32, (64, C), 1)
    zs[...] = jnp.where(lane >= 40 * ((4 * m + 5 * r) & 7), pair[0:64], pair[64:128])
    slots[...] = jnp.zeros(slots.shape, F32)
    for i in range(64):
        slots[i, 7:8, :] = zs[i : i + 1, :]

    swapped(fg2, 3)
    whole = flat(fg2[...])
    wide = whole.astype(F32)
    fgs[1] = whole
    fgs[0] = moved(wide, -1).astype(BF16)
    fgs[2] = moved(wide, 1).astype(BF16)
    for tap in range(5):
        column = jnp.where(zero, tap % 3, (4 + tap) % 3)
        start = jnp.where(zero, FIRST_SLOTS[0][tap], FIRST_SLOTS[1][tap])
        slots[pl.ds(start, 16)] += mm(xsel[tap], fgs[column]).reshape(16, NR, C)

    @pl.when(zero)
    def _():
        for a in range(NR):
            rsb[a] = jnp.concatenate([slots[NR * b + a] for b in range(NR)], axis=0).astype(BF16)

    @pl.when(s == 1)
    def _():
        for a in range(NR):
            rsb[a] = jnp.concatenate([slots[NR * a + b] for b in range(NR)], axis=0).astype(BF16)

    for k in FAR:
        push(rsb.at[ring(pa, k)], rsr.at[k], r1_s.at[k], r1_r.at[k], dev(k, 0))
    total = rsb[pa].astype(F32)
    for k in range(1, NR):
        arrived(rsr.at[k], r1_s.at[k], r1_r.at[k])
        total = total + rsr[k].astype(F32)
    s2b[...] = total.reshape(NR, NR, C)
    for k in FAR:
        push(s2b.at[ring(pb, k)], s2r.at[k], r2_s.at[k], r2_r.at[k], dev(0, k))
    total = s2b[pb]
    for k in range(1, NR):
        arrived(s2r.at[k], r2_s.at[k], r2_r.at[k])
        total = total + s2r[k]
    off = 40 * ((4 * d + 5 * r) & 7)
    wide = jnp.concatenate([total, jnp.zeros((NR, WIDE - C), F32)], axis=1)
    after = jnp.where(lax.broadcasted_iota(jnp.int32, wide.shape, 0) == 7, wide, pltpu.roll(wide, 7, 0))
    lane = lax.broadcasted_iota(jnp.int32, wide.shape, 1)
    wide = jnp.where(lane < C - off, pltpu.roll(wide, lax.rem(WIDE - off, WIDE), 1), pltpu.roll(after, C - off, 1))
    out_ref[...] = wide[:, 0:C]
    for copy in sends:
        copy.wait_send()


def per_device(latent, hint, decoder_in, target, first_convs, second_convs, pointwise):
    vm = pltpu.VMEM
    dma = pltpu.SemaphoreType.DMA
    image = (ROWS + 2, WC, C)
    cells = (CELLS, C)
    scratch = [vm((2, NR, NR) + block, BF16) for block in BLOCKS]
    scratch += [
        vm((2, 3, 9 * C, C), BF16), vm((2, 2, C, C), BF16), vm((728, C), F32), vm((2, 48, C), F32), vm((2, C, C), F32),
        vm((3, 64, WIDE), F32), vm((4,) + image, BF16), vm((2,) + image, BF16), vm((2,) + cells, BF16), vm((2,) + cells, BF16),
        vm((2,) + cells, BF16), vm(cells, F32), vm(cells, F32), vm(cells, F32),
        vm(image, BF16), vm(image, BF16), vm(image, BF16), vm(image, BF16),
        vm((5, 128, 2 * CELLS), BF16), vm((3, 2 * CELLS, C), BF16), vm((64, C), F32),
        vm((64, NR, C), F32), vm((NR, 64, C), BF16), vm((NR, 64, C), BF16), vm((NR, NR, C), F32), vm((NR, NR, C), F32),
    ]
    for shape in ((3, 2, 4), (3, 2, 2, 4), (3, 2, 4), (3, 5), (2, 2), (4,), (NR,), (NR,)):
        scratch += [dma(shape), dma(shape)]
    scratch += [dma((4,))]
    got = pl.pallas_call(
        kernel,
        out_shape=jax.ShapeDtypeStruct((8, C), F32),
        in_specs=[pl.BlockSpec(memory_space=pl.ANY)] * 4 + [pl.BlockSpec(memory_space=pltpu.VMEM)] * 3,
        out_specs=pl.BlockSpec(memory_space=pltpu.VMEM),
        scratch_shapes=scratch,
        compiler_params=pltpu.CompilerParams(
            collective_id=0, has_side_effects=True, vmem_limit_bytes=60 * 1024 * 1024
        ),
        name="step",
    )(latent, hint, decoder_in, target, jnp.swapaxes(first_convs[0], 0, 1), second_convs, jnp.swapaxes(pointwise[0], 0, 1))
    return got[:6].reshape(-1)[:1800], got[7, :200]


def solution(mesh):
    placed = (
        P("dp", "rows", None, None),
        P("dp", "rows", None, None),
        P("dp", "rows", None, None),
        P("dp", "rows", None, None),
        P("segment", None, "dp", None),
        P("segment", "dp", None),
        P("segment", None, "dp", None),
    )
    return jax.shard_map(
        per_device,
        mesh=mesh,
        in_specs=placed,
        out_specs=(P(("segment", "dp", "rows")), P(("segment", "dp", "rows"))),
        check_vma=False,
    )
```
